128 devices in a mesh: px: 32 (over z, x, core), vx: 4 (over y).
Axes of the slice: x: 4, y: 4, z: 4, core: 2. Of those that a mesh axis runs over, the one named last changes fastest.
Arguments:
- value_field: float32 [64, 96, 64, 384], P('px', 'vx'), may hold values from -6 to 6
- cost_field: float32 [64, 96, 64, 384], P('px', 'vx'), may hold values from -6 to 6
- accel_first: float32 [64, 96], P('px', 'vx'), may hold values from -3 to 3
- accel_second: float32 [64, 384], replicated, may hold values from -1 to 1
Outputs:
- final_value: float32 [64, 96, 64, 384], P('px', 'vx')
- funnel_slice: float32 [64, 384], P('px')
The draws below stay inside these ranges and needn't reach their ends.
All inputs are finite; a program needn't handle non-finite values.
Results may differ from the reference program's by a relative error of at most 0.00002.
Values sent between devices are 32-bit elements; how exact they have to be, the bound alone decides.
A program may use at most 128 MiB of HBM per device.

```python
import jax
import jax.numpy as jnp
from jax import lax

NVY = 64
NY = 384
NX = 64
NVX = 96


def draw_accel_first(key, part):
    rise = 1.0 + 2.0 * jnp.arange(NX, dtype=jnp.float32) / max(NX - 1, 1)
    base = jax.random.uniform(key, (NX, NVX), jnp.float32, -1.0, 1.0)
    return base * rise[:, None]


def shard_levels(stream_key, dims, shards, low, top_value):
    def one(position, blocks):
        steps = jax.random.uniform(jax.random.fold_in(jax.random.fold_in(stream_key, 6), position), (blocks,), jnp.float32, low / len(shards), top_value / len(shards))
        return jnp.repeat(jnp.exp(steps), dims[position] // blocks).reshape((-1,) + (1,) * (len(dims) - position - 1))

    loudness = one(*shards[0])
    for cut in shards[1:]:
        loudness = loudness * one(*cut)
    return loudness


def noise(rng, dims, scale, limit, pieces=(), kind=jnp.bfloat16):
    drawn = scale * jax.random.normal(rng, dims, jnp.float32)
    if pieces:
        drawn = drawn * shard_levels(rng, dims, pieces, -0.22, 0.18)
    return jnp.clip(drawn, -limit, limit).astype(kind)


def setup_inputs(seed: int = 0) -> dict:
    splits = jax.random.split(jax.random.key(seed), 5)
    return {
        "value_field": noise(splits[0], (NX, NVX, NVY, NY), 1.0, 6.0, ((0, 32), (1, 4)), jnp.float32),
        "cost_field": noise(splits[1], (NX, NVX, NVY, NY), 1.0, 6.0, ((0, 32), (1, 4)), jnp.float32),
        "accel_first": draw_accel_first(jax.random.fold_in(splits[4], 71), 0),
        "accel_second": jnp.clip(jax.random.uniform(splits[3], (NVY, NY), jnp.float32, -1.0, 1.0), -1.0, 1.0),
    }


VELOCITY_LIMIT = 1.0
PLANNER_SPEED = 0.3
DISTURBANCE = 0.2
CONTROL_COST = 1.0
COURANT = 0.5


def interior(padded, dimension, offset):
    index_list = []
    for axis_number in range(4):
        size_here = padded.shape[axis_number]
        if axis_number == dimension:
            index_list.append(slice(1 + offset, size_here - 1 + offset))
        else:
            index_list.append(slice(1, size_here - 1))
    return padded[tuple(index_list)]


def slopes(padded, spacings):
    center = interior(padded, 0, 0)
    gradients = []
    curvatures = []
    for dimension in range(4):
        upper = interior(padded, dimension, 1)
        lower = interior(padded, dimension, -1)
        gradients.append((upper - lower) / (2.0 * spacings[dimension]))
        curvatures.append((upper - 2.0 * center + lower) / spacings[dimension])
    return center, gradients, curvatures


def hamiltonian(gradients, curvatures, speed_first, speed_second, push_first, push_second, rates):
    total = gradients[0] * speed_first + gradients[3] * speed_second
    total = total + PLANNER_SPEED * (jnp.abs(gradients[0]) + jnp.abs(gradients[3]))
    total = total + gradients[1] * push_first + gradients[2] * push_second
    total = total + DISTURBANCE * (jnp.abs(gradients[1]) + jnp.abs(gradients[2]))
    total = total - (gradients[1] * gradients[1] + gradients[2] * gradients[2]) / (2.0 * CONTROL_COST)
    damping = rates[0] * curvatures[0] + rates[1] * curvatures[1] + rates[2] * curvatures[2] + rates[3] * curvatures[3]
    return total - 0.5 * damping


def reference(value_field, cost_field, accel_first, accel_second):
    speed_first = ((2.0 * jnp.arange(NVX, dtype=jnp.float32) + 1.0 - NVX) * (VELOCITY_LIMIT / NVX)).reshape(NVX, 1, 1)
    speed_second = ((2.0 * jnp.arange(NVY, dtype=jnp.float32) + 1.0 - NVY) * (VELOCITY_LIMIT / NVY)).reshape(NVY, 1)
    velocity_step_x = 2.0 * VELOCITY_LIMIT / NVX
    velocity_step_y = 2.0 * VELOCITY_LIMIT / NVY
    position_step = velocity_step_x * velocity_step_y
    spacings = (position_step, velocity_step_x, velocity_step_y, position_step)
    push_limit = jnp.max(jnp.abs(accel_first))
    push_second_limit = jnp.max(jnp.abs(accel_second))
    rate_first = VELOCITY_LIMIT * (NVX - 1) / NVX + PLANNER_SPEED
    rate_last = VELOCITY_LIMIT * (NVY - 1) / NVY + PLANNER_SPEED
    indices = jnp.arange(NX, dtype=jnp.int32)

    def rates_of(padded):
        def row_maxima(index):
            block = lax.dynamic_slice_in_dim(padded, index, 3, 0)
            center, gradients, curvatures = slopes(block, spacings)
            return jnp.max(jnp.abs(gradients[1])), jnp.max(jnp.abs(gradients[2]))
        first_max, second_max = lax.map(row_maxima, indices)
        return (rate_first, push_limit + DISTURBANCE + jnp.max(first_max) / CONTROL_COST,
                push_second_limit + DISTURBANCE + jnp.max(second_max) / CONTROL_COST, rate_last)

    def sweep(padded, rates, step_size, base):
        def row_update(index):
            block = lax.dynamic_slice_in_dim(padded, index, 3, 0)
            center, gradients, curvatures = slopes(block, spacings)
            push_row = lax.dynamic_slice_in_dim(accel_first, index, 1, 0).reshape(1, NVX, 1, 1)
            change = hamiltonian(gradients, curvatures, speed_first, speed_second, push_row, accel_second, rates)
            cost_row = lax.dynamic_slice_in_dim(cost_field, index, 1, 0)
            moved = center + step_size * change
            if base is not None:
                base_row = lax.dynamic_slice_in_dim(base, index, 1, 0)
                moved = 0.5 * base_row + 0.5 * moved
            return jnp.maximum(cost_row, moved)[0]
        return lax.map(row_update, indices)

    current = value_field
    for repeat in range(2):
        padded = jnp.pad(current, 1, mode="edge")
        rates = rates_of(padded)
        step_size = COURANT / (rates[0] / spacings[0] + rates[1] / spacings[1] + rates[2] / spacings[2] + rates[3] / spacings[3])
        middle = sweep(padded, rates, step_size, None)
        padded = jnp.pad(middle, 1, mode="edge")
        rates = rates_of(padded)
        current = sweep(padded, rates, step_size, current)
    return current, jnp.min(current, axis=(1, 2))
```

```python
import functools

import jax
import jax.numpy as jnp
from jax import lax
from jax.experimental import pallas as pl
from jax.experimental.pallas import tpu as pltpu
from jax.sharding import PartitionSpec as P

MESH = pl.DeviceIdType.MESH
VELOCITY_LIMIT = 1.0
PLANNER_SPEED = 0.3
DISTURBANCE = 0.2
CONTROL_COST = 1.0
COURANT = 0.5
CHUNK = 1
RING = 4


def kernel(
    a1_s,
    a1_v,
    value,
    cost_hbm,
    a2_hbm,
    out,
    funnel,
    f0,
    f1,
    f2,
    f3,
    cost,
    a2,
    tab_v,
    tab_a,
    red_s,
    red_r,
    coef,
    fun_s,
    fun_r,
    px_send,
    px_recv,
    vx_send,
    vx_recv,
    red_send,
    red_recv,
    fun_send,
    fun_recv,
    load_sem,
):
    fields = (f0, f1, f2, f3)
    rows = cost.shape[1]
    tall = cost.shape[2]
    wide = cost.shape[3]
    strips = tall // 8
    tiles = wide // 128
    chunks = rows // CHUNK
    px, vx = lax.axis_index("px"), lax.axis_index("vx")
    npx, nvx = lax.axis_size("px"), lax.axis_size("vx")
    total_vx = rows * nvx
    h2 = 2.0 * VELOCITY_LIMIT / total_vx
    h3 = 2.0 * VELOCITY_LIMIT / tall
    h1 = h2 * h3
    r1 = VELOCITY_LIMIT * (total_vx - 1) / total_vx + PLANNER_SPEED
    r4 = VELOCITY_LIMIT * (tall - 1) / tall + PLANNER_SPEED

    core = px % 2
    chip_x = (px // 2) % RING
    chip_z = px // (2 * RING)
    has_left, has_right = px > 0, px < npx - 1
    has_down, has_up = vx > 0, vx < nvx - 1
    first_p = (npx - 1 - px) // (npx - 1)
    last_p = px // (npx - 1)
    first_v = (nvx - 1 - vx) // (nvx - 1)
    last_v = vx // (nvx - 1)
    plane_low = first_p
    plane_high = 3 - last_p

    def ring_device(axis, step, which):
        if axis == "z":
            return (((chip_z + step) % RING * RING + chip_x) * 2 + which, vx)
        if axis == "x":
            return ((chip_z * RING + (chip_x + step) % RING) * 2 + which, vx)
        return ((chip_z * RING + chip_x) * 2 + which, (vx + step) % RING)

    partner = (px + 1 - 2 * core, vx)

    load_value = pltpu.make_async_copy(
        value, f0.at[pl.ds(1, 2), pl.ds(1, rows)], load_sem.at[0]
    )
    load_cost = pltpu.make_async_copy(cost_hbm, cost, load_sem.at[1])
    load_a2 = pltpu.make_async_copy(a2_hbm, a2, load_sem.at[2])
    load_value.start()

    barrier = pltpu.get_barrier_semaphore()

    def greet(device):
        pl.semaphore_signal(barrier, inc=1, device_id=device, device_id_type=MESH)

    greet(partner)
    for axis in ("x", "y", "z"):
        for step in range(1, RING):
            for which in (0, 1):
                greet(ring_device(axis, step, which))
    far_left = jnp.logical_and(jnp.logical_and(core == 0, chip_x == 0), has_left)
    far_right = jnp.logical_and(
        jnp.logical_and(core == 1, chip_x == RING - 1), has_right
    )

    @pl.when(far_left)
    def _():
        greet((px - 1, vx))

    @pl.when(far_right)
    def _():
        greet((px + 1, vx))

    far = far_left.astype(jnp.int32) + far_right.astype(jnp.int32)
    pl.semaphore_wait(barrier, 1 + 3 * 2 * (RING - 1) + far)

    def px_copy(stage, side, chunk):
        dst_plane = 3 if side == 0 else 0
        span = pl.ds(chunk * CHUNK + 1, CHUNK)
        if stage == 0:
            src = value.at[side, pl.ds(chunk * CHUNK, CHUNK)]
        else:
            src = fields[stage].at[1 + side, span]
        return pltpu.make_async_remote_copy(
            src_ref=src,
            dst_ref=fields[stage].at[dst_plane, span],
            send_sem=px_send.at[stage, side, chunk],
            recv_sem=px_recv.at[stage, side, chunk],
            device_id=(px - 1 if side == 0 else px + 1, vx),
            device_id_type=MESH,
        )

    def px_start(stage, chunk):
        @pl.when(has_left)
        def _():
            px_copy(stage, 0, chunk).start()

        @pl.when(has_right)
        def _():
            px_copy(stage, 1, chunk).start()

    def px_wait_send(stage, chunk):
        @pl.when(has_left)
        def _():
            px_copy(stage, 0, chunk).wait_send()

        @pl.when(has_right)
        def _():
            px_copy(stage, 1, chunk).wait_send()

    def px_wait_recv(stage, chunk):
        @pl.when(has_left)
        def _():
            px_copy(stage, 1, chunk).wait_recv()

        @pl.when(has_right)
        def _():
            px_copy(stage, 0, chunk).wait_recv()

    def vx_copy(stage, side):
        src_row = 1 if side == 0 else rows
        dst_row = rows + 1 if side == 0 else 0
        if stage == 0:
            src = value.at[:, pl.ds(src_row - 1, 1)]
        else:
            src = fields[stage].at[pl.ds(1, 2), pl.ds(src_row, 1)]
        return pltpu.make_async_remote_copy(
            src_ref=src,
            dst_ref=fields[stage].at[pl.ds(1, 2), pl.ds(dst_row, 1)],
            send_sem=vx_send.at[stage, side],
            recv_sem=vx_recv.at[stage, side],
            device_id=(px, vx - 1 if side == 0 else vx + 1),
            device_id_type=MESH,
        )

    def vx_start(stage):
        @pl.when(has_down)
        def _():
            vx_copy(stage, 0).start()

        @pl.when(has_up)
        def _():
            vx_copy(stage, 1).start()

    def vx_wait(stage):
        @pl.when(has_down)
        def _():
            vx_copy(stage, 0).wait_send()
            vx_copy(stage, 1).wait_recv()

        @pl.when(has_up)
        def _():
            vx_copy(stage, 1).wait_send()
            vx_copy(stage, 0).wait_recv()

    def chunk_order(index):
        return (index + chunks - 1) % chunks

    vx_start(0)

    @pl.loop(0, chunks)
    def _(index):
        px_start(0, chunk_order(index))

    load_cost.start()
    load_a2.start()

    sub = lax.broadcasted_iota(jnp.int32, (8, 128), 0)
    lane = lax.broadcasted_iota(jnp.int32, (8, 128), 1)
    sub_first, sub_last = sub == 0, sub == 7
    lane_first, lane_last = lane == 0, lane == 127

    load_a2.wait()
    a2_peak = jnp.max(jnp.abs(a2[...]), keepdims=True)
    a1_peak = jnp.max(jnp.abs(a1_v[...]), keepdims=True)
    load_value.wait()

    def ring_copy(stage, hop, axis, step, which, slot, send_slot):
        return pltpu.make_async_remote_copy(
            src_ref=red_s.at[stage, hop],
            dst_ref=red_r.at[stage, hop, slot],
            send_sem=red_send.at[stage, hop, send_slot],
            recv_sem=red_recv.at[stage, hop, slot],
            device_id=ring_device(axis, step, which),
            device_id_type=MESH,
        )

    def pair_copy(stage):
        return pltpu.make_async_remote_copy(
            src_ref=red_s.at[stage, 0],
            dst_ref=red_r.at[stage, 0, 0],
            send_sem=red_send.at[stage, 0, 0],
            recv_sem=red_recv.at[stage, 0, 0],
            device_id=partner,
            device_id_type=MESH,
        )

    axes = ("y", "z", "x")

    def all_max(stage, mine):
        red_s[stage, 0] = mine
        pair_copy(stage).start()
        pair_copy(stage).wait_recv()
        best = jnp.maximum(red_s[stage, 0], red_r[stage, 0, 0])
        for hop, axis in enumerate(axes, 1):
            red_s[stage, hop] = best

            @pl.when(core == 0)
            def _():
                for which in (0, 1):
                    ring_copy(stage, hop, axis, 1, which, 0, which).start()
                for which in (0, 1):
                    ring_copy(stage, hop, axis, 2, which, 1, 2 + which).start()

            @pl.when(core == 1)
            def _():
                for which in (0, 1):
                    ring_copy(stage, hop, axis, RING - 1, which, 2, which).start()

            for slot in range(3):
                ring_copy(stage, hop, axis, 1, 0, slot, 0).wait_recv()
            best = jnp.maximum(
                jnp.maximum(red_s[stage, hop], red_r[stage, hop, 0]),
                jnp.maximum(red_r[stage, hop, 1], red_r[stage, hop, 2]),
            )
        return best

    def all_max_drain(stage):
        pair_copy(stage).wait_send()
        for hop, axis in enumerate(axes, 1):

            @pl.when(core == 0)
            def _():
                for which in (0, 1):
                    ring_copy(stage, hop, axis, 1, which, 0, which).wait_send()
                    ring_copy(stage, hop, axis, 2, which, 1, 2 + which).wait_send()

            @pl.when(core == 1)
            def _():
                for which in (0, 1):
                    ring_copy(stage, hop, axis, RING - 1, which, 2, which).wait_send()

    def row_neighbours(row):
        here = row + 1
        down = row + first_v * ((rows - 1 - row) // (rows - 1))
        up = row + 2 - last_v * (row // (rows - 1))
        return here, down, up

    def tile(s, c):
        return pl.ds(8 * s, 8), pl.ds(128 * c, 128)

    def local_maxima(field):
        def body(row, carry):
            here, down, up = row_neighbours(row)
            m2, m3 = carry
            for plane in (1, 2):
                for c in range(tiles):
                    cells = [field[(plane, here) + tile(s, c)] for s in range(strips)]
                    turned = [pltpu.roll(x, 6, 0) for x in cells]
                    for s in range(strips):
                        above = field[(plane, up) + tile(s, c)]
                        below = field[(plane, down) + tile(s, c)]
                        m2 = jnp.maximum(m2, jnp.abs(above - below))
                        if s < strips - 1:
                            ahead = jnp.where(sub >= 6, turned[s + 1], turned[s])
                        else:
                            ahead = jnp.where(sub >= 6, cells[s], turned[s])
                        m3 = jnp.maximum(m3, jnp.abs(ahead - cells[s]))
                    step = jnp.abs(pltpu.roll(cells[0], 7, 0) - cells[0])
                    m3 = jnp.maximum(m3, jnp.where(sub_first, step, 0.0))
                    step = jnp.abs(pltpu.roll(cells[-1], 7, 0) - cells[-1])
                    m3 = jnp.maximum(m3, jnp.where(sub == 6, step, 0.0))
            return m2, m3

        zero = jnp.zeros((8, 128), jnp.float32)
        m2, m3 = lax.fori_loop(0, rows, body, (zero, zero))
        return jnp.max(m2, keepdims=True), jnp.max(m3, keepdims=True)

    def spread(x):
        return jnp.broadcast_to(x, (8, 128))

    def make_coefficients(stage, best):
        m2, m3 = spread(best[0:1]), spread(best[1:2])
        push_limit = spread(best[2:3])
        if stage == 0:
            coef[7] = push_limit
        else:
            push_limit = coef[7]
        r2 = push_limit + (DISTURBANCE) + m2 * (1.0 / (2.0 * h2 * CONTROL_COST))
        r3 = (
            spread(a2_peak) + (DISTURBANCE) + m3 * (1.0 / (2.0 * h3 * CONTROL_COST))
        )
        courant = r1 / h1 + r2 / h2 + r3 / h3 + r4 / h1
        if stage % 2 == 0:
            dt = COURANT / courant
            coef[6] = dt
            centre = 1.0 + dt * courant
            scale = dt
        else:
            dt = coef[6]
            centre = 0.5 + 0.5 * (dt * courant)
            scale = 0.5 * dt
        k1 = scale * (1.0 / (2.0 * h1))
        k2 = scale * (1.0 / (2.0 * h2))
        k3 = scale * (1.0 / (2.0 * h3))
        coef[0] = k1
        coef[1] = k2
        coef[2] = k2 * r2
        coef[3] = k3 * (1.0 / (4.0 * h3 * CONTROL_COST))
        coef[4] = k3 * r3
        coef[5] = centre
        for s in range(strips):
            speed = (
                (2 * (sub + 8 * s) + 1 - tall).astype(jnp.float32)
                * (VELOCITY_LIMIT / tall)
            )
            tab_v[0, pl.ds(8 * s, 8)] = k1 * (speed + PLANNER_SPEED)
            tab_v[1, pl.ds(8 * s, 8)] = k1 * (speed - PLANNER_SPEED)
            for c in range(tiles):
                push = a2[tile(s, c)]
                tab_a[(0,) + tile(s, c)] = k3 * (push + DISTURBANCE)
                tab_a[(1,) + tile(s, c)] = k3 * (push - DISTURBANCE)

    def update_row(stage, row):
        field = fields[stage]
        here, down, up = row_neighbours(row)
        k1, k2 = coef[0], coef[1]
        e1, e4 = k1 * r1, k1 * r4
        q2 = k2 * (1.0 / (4.0 * h2 * CONTROL_COST))
        e2, q3, e3, centre = coef[2], coef[3], coef[4], coef[5]
        speed = (2 * (vx * rows + row) + 1 - total_vx).astype(jnp.float32) * (
            VELOCITY_LIMIT / total_vx
        )
        p1 = k1 * (speed + PLANNER_SPEED)
        n1 = k1 * (speed - PLANNER_SPEED)
        for plane in (1, 2):
            left = plane_low if plane == 1 else 1
            right = 2 if plane == 1 else plane_high
            push = a1_s[plane - 1, row]
            p2 = k2 * (push + DISTURBANCE)
            n2 = k2 * (push - DISTURBANCE)
            cells, ahead, behind = {}, {}, {}

            def fetch(s):
                for c in range(tiles):
                    x = field[(plane, here) + tile(s, c)]
                    cells[s, c] = x
                    ahead[s, c] = pltpu.roll(x, 7, 0)
                    behind[s, c] = pltpu.roll(x, 1, 0)

            fetch(0)
            for s in range(strips):
                if s + 1 < strips:
                    fetch(s + 1)
                lefts = [pltpu.roll(cells[s, c], 1, 1) for c in range(tiles)]
                rights = [pltpu.roll(cells[s, c], 127, 1) for c in range(tiles)]
                v_plus = tab_v[0, pl.ds(8 * s, 8)]
                v_minus = tab_v[1, pl.ds(8 * s, 8)]
                for c in range(tiles):
                    x = cells[s, c]
                    hi = field[(right, here) + tile(s, c)]
                    lo = field[(left, here) + tile(s, c)]
                    d = hi - lo
                    total = jnp.maximum(d * p1, d * n1) - e1 * (hi + lo)
                    hi = jnp.where(
                        lane_last, rights[c + 1] if c + 1 < tiles else x, rights[c]
                    )
                    lo = jnp.where(lane_first, lefts[c - 1] if c > 0 else x, lefts[c])
                    d = hi - lo
                    total += jnp.maximum(d * v_plus, d * v_minus) - e4 * (hi + lo)
                    hi = field[(plane, up) + tile(s, c)]
                    lo = field[(plane, down) + tile(s, c)]
                    d = hi - lo
                    total += d * (jnp.where(d > 0, p2, n2) - q2 * d) - e2 * (hi + lo)
                    hi = jnp.where(
                        sub_last,
                        ahead[s + 1, c] if s + 1 < strips else x,
                        ahead[s, c],
                    )
                    lo = jnp.where(
                        sub_first, behind[s - 1, c] if s > 0 else x, behind[s, c]
                    )
                    d = hi - lo
                    p3 = tab_a[(0,) + tile(s, c)]
                    n3 = tab_a[(1,) + tile(s, c)]
                    total += d * (jnp.where(d > 0, p3, n3) - q3 * d) - e3 * (hi + lo)
                    moved = centre * x + total
                    floor = cost[(plane - 1, row) + tile(s, c)]
                    if stage % 2 == 1:
                        base = fields[stage - 1][(plane, here) + tile(s, c)]
                        moved = 0.5 * base + moved
                    result = jnp.maximum(floor, moved)
                    if stage == 3:
                        out[(plane - 1, row) + tile(s, c)] = result
                        slot = plane - 1, slice(None), pl.ds(128 * c, 128)
                        fun_s[slot] = jnp.minimum(fun_s[slot], result)
                    else:
                        fields[stage + 1][(plane, here) + tile(s, c)] = result

    fun_s[...] = jnp.full(fun_s.shape, jnp.inf, jnp.float32)

    for stage in range(4):
        vx_wait(stage)
        m2, m3 = local_maxima(fields[stage])
        mine = jnp.where(sub == 0, spread(m2), jnp.where(sub == 1, spread(m3), spread(a1_peak)))
        best = all_max(stage, mine)
        make_coefficients(stage, best)
        if stage == 0:
            load_cost.wait()

        @pl.loop(0, chunks)
        def _(index):
            chunk = chunk_order(index)
            px_wait_recv(stage, chunk)
            if stage > 0:
                px_wait_send(stage - 1, chunk)

            @pl.loop(0, CHUNK)
            def _(k):
                update_row(stage, chunk * CHUNK + k)

            if stage < 3:

                @pl.when(index > 0)
                def _():
                    px_start(stage + 1, chunk_order(index - 1))

        if stage < 3:
            px_start(stage + 1, chunk_order(chunks - 1))
            vx_start(stage + 1)
        all_max_drain(stage)

    def funnel_copy(step):
        return pltpu.make_async_remote_copy(
            src_ref=fun_s,
            dst_ref=fun_r.at[step - 1],
            send_sem=fun_send.at[step - 1],
            recv_sem=fun_recv.at[step - 1],
            device_id=(px, (vx + step) % nvx),
            device_id_type=MESH,
        )

    for step in range(1, RING):
        funnel_copy(step).start()

    @pl.loop(0, chunks)
    def _(index):
        px_wait_send(3, index)

    least = fun_s[...]
    for step in range(1, RING):
        funnel_copy(step).wait_recv()
        least = jnp.minimum(least, fun_r[step - 1])
    funnel[...] = jnp.min(least, axis=1)
    for step in range(1, RING):
        funnel_copy(step).wait_send()


def per_device(value_field, cost_field, accel_first, accel_second):
    cells_x, rows, tall, wide = value_field.shape
    field = pltpu.VMEM((cells_x + 2, rows + 2, tall, wide), jnp.float32)
    chunks = rows // CHUNK
    dma = pltpu.SemaphoreType.DMA
    hbm = pl.BlockSpec(memory_space=pl.ANY)
    vmem = pl.BlockSpec(memory_space=pltpu.VMEM)
    return pl.pallas_call(
        kernel,
        out_shape=(
            pltpu.VMEM(value_field.shape, jnp.float32),
            pltpu.VMEM((cells_x, wide), jnp.float32),
        ),
        in_specs=[pl.BlockSpec(memory_space=pltpu.SMEM), vmem, hbm, hbm, hbm],
        out_specs=(vmem, vmem),
        scratch_shapes=[
            field,
            field,
            field,
            field,
            pltpu.VMEM((cells_x, rows, tall, wide), jnp.float32),
            pltpu.VMEM((tall, wide), jnp.float32),
            pltpu.VMEM((2, tall, 128), jnp.float32),
            pltpu.VMEM((2, tall, wide), jnp.float32),
            pltpu.VMEM((4, 4, 8, 128), jnp.float32),
            pltpu.VMEM((4, 4, 3, 8, 128), jnp.float32),
            pltpu.VMEM((8, 8, 128), jnp.float32),
            pltpu.VMEM((cells_x, 8, wide), jnp.float32),
            pltpu.VMEM((RING - 1, cells_x, 8, wide), jnp.float32),
            dma((4, 2, chunks)),
            dma((4, 2, chunks)),
            dma((4, 2)),
            dma((4, 2)),
            dma((4, 4, 4)),
            dma((4, 4, 3)),
            dma((RING - 1,)),
            dma((RING - 1,)),
            dma((3,)),
        ],
        compiler_params=pltpu.CompilerParams(
            collective_id=0, has_side_effects=True, vmem_limit_bytes=56 * 1000 * 1000
        ),
    )(accel_first, accel_first, value_field, cost_field, accel_second)


def solution(mesh):
    placed = (P("px", "vx", None, None), P("px", "vx", None, None), P("px", "vx"), P())
    return jax.shard_map(
        per_device,
        mesh=mesh,
        in_specs=placed,
        out_specs=(P("px", "vx", None, None), P("px", None)),
        check_vma=False,
    )
```

```python
import functools

import jax
import jax.numpy as jnp
from jax import lax
from jax.experimental import pallas as pl
from jax.experimental.pallas import tpu as pltpu
from jax.sharding import PartitionSpec as P

MESH = pl.DeviceIdType.MESH
VELOCITY_LIMIT = 1.0
PLANNER_SPEED = 0.3
DISTURBANCE = 0.2
CONTROL_COST = 1.0
COURANT = 0.5
CHUNK = 2
RING = 4


def kernel(
    a1_s,
    a1_v,
    value,
    cost_hbm,
    a2_hbm,
    out,
    funnel,
    f0,
    f1,
    f2,
    f3,
    cost,
    a2,
    tab_v,
    tab_a,
    red_s,
    red_r,
    peak,
    coef,
    fun_s,
    fun_r,
    px_send,
    px_recv,
    vx_send,
    vx_recv,
    red_send,
    red_recv,
    fun_send,
    fun_recv,
    load_sem,
):
    fields = (f0, f1, f2, f3)
    rows = cost.shape[1]
    tall = cost.shape[2]
    wide = cost.shape[3]
    strips = tall // 8
    tiles = wide // 128
    chunks = rows // CHUNK
    px, vx = lax.axis_index("px"), lax.axis_index("vx")
    npx, nvx = lax.axis_size("px"), lax.axis_size("vx")
    total_vx = rows * nvx
    h2 = 2.0 * VELOCITY_LIMIT / total_vx
    h3 = 2.0 * VELOCITY_LIMIT / tall
    h1 = h2 * h3
    r1 = VELOCITY_LIMIT * (total_vx - 1) / total_vx + PLANNER_SPEED
    r4 = VELOCITY_LIMIT * (tall - 1) / tall + PLANNER_SPEED

    core = px % 2
    chip_x = (px // 2) % RING
    chip_z = px // (2 * RING)
    has_left, has_right = px > 0, px < npx - 1
    has_down, has_up = vx > 0, vx < nvx - 1
    first_p = (npx - 1 - px) // (npx - 1)
    last_p = px // (npx - 1)
    first_v = (nvx - 1 - vx) // (nvx - 1)
    last_v = vx // (nvx - 1)
    plane_low = first_p
    plane_high = 3 - last_p

    def chip_device(x, y, z, which):
        return ((z * RING + x) * 2 + which, y)

    def across(which):
        return chip_device(chip_x + 1 - 2 * (chip_x % 2), vx, chip_z, which)

    def mirror(which):
        return chip_device(RING - 1 - chip_x, vx, chip_z, which)

    def along_y(step, which):
        return chip_device(chip_x, (vx + step) % RING, chip_z, which)

    def along_z(step):
        return chip_device(chip_x, vx, (chip_z + step) % RING, core)

    partner = (px + 1 - 2 * core, vx)

    load_value = pltpu.make_async_copy(
        value, f0.at[pl.ds(1, 2), pl.ds(1, rows)], load_sem.at[0]
    )
    load_cost = pltpu.make_async_copy(cost_hbm, cost, load_sem.at[1])
    load_a2 = pltpu.make_async_copy(a2_hbm, a2, load_sem.at[2])
    load_value.start()

    barrier = pltpu.get_barrier_semaphore()

    def greet(device):
        pl.semaphore_signal(barrier, inc=1, device_id=device, device_id_type=MESH)

    greet(partner)
    for which in (0, 1):
        greet(across(which))
        greet(mirror(which))
    for step in range(1, RING):
        greet(along_y(step, 0))
        greet(along_y(step, 1))
        greet(along_z(step))
    far_left = jnp.logical_and(jnp.logical_and(core == 0, chip_x == 0), has_left)
    far_right = jnp.logical_and(
        jnp.logical_and(core == 1, chip_x == RING - 1), has_right
    )

    @pl.when(far_left)
    def _():
        greet((px - 1, vx))

    @pl.when(far_right)
    def _():
        greet((px + 1, vx))

    far = far_left.astype(jnp.int32) + far_right.astype(jnp.int32)
    pl.semaphore_wait(barrier, 5 + 3 * (RING - 1) + far)

    def px_copy(stage, side, chunk):
        dst_plane = 3 if side == 0 else 0
        span = pl.ds(chunk * CHUNK + 1, CHUNK)
        if stage == 0:
            src = value.at[side, pl.ds(chunk * CHUNK, CHUNK)]
        else:
            src = fields[stage].at[1 + side, span]
        return pltpu.make_async_remote_copy(
            src_ref=src,
            dst_ref=fields[stage].at[dst_plane, span],
            send_sem=px_send.at[stage, side, chunk],
            recv_sem=px_recv.at[stage, side, chunk],
            device_id=(px - 1 if side == 0 else px + 1, vx),
            device_id_type=MESH,
        )

    def px_start(stage, chunk):
        @pl.when(has_left)
        def _():
            px_copy(stage, 0, chunk).start()

        @pl.when(has_right)
        def _():
            px_copy(stage, 1, chunk).start()

    def px_wait_send(stage, chunk):
        @pl.when(has_left)
        def _():
            px_copy(stage, 0, chunk).wait_send()

        @pl.when(has_right)
        def _():
            px_copy(stage, 1, chunk).wait_send()

    def px_wait_recv(stage, chunk):
        @pl.when(has_left)
        def _():
            px_copy(stage, 1, chunk).wait_recv()

        @pl.when(has_right)
        def _():
            px_copy(stage, 0, chunk).wait_recv()

    def vx_copy(stage, side):
        src_row = 1 if side == 0 else rows
        dst_row = rows + 1 if side == 0 else 0
        if stage == 0:
            src = value.at[:, pl.ds(src_row - 1, 1)]
        else:
            src = fields[stage].at[pl.ds(1, 2), pl.ds(src_row, 1)]
        return pltpu.make_async_remote_copy(
            src_ref=src,
            dst_ref=fields[stage].at[pl.ds(1, 2), pl.ds(dst_row, 1)],
            send_sem=vx_send.at[stage, side],
            recv_sem=vx_recv.at[stage, side],
            device_id=(px, vx - 1 if side == 0 else vx + 1),
            device_id_type=MESH,
        )

    def vx_start(stage, side):
        @pl.when(has_down if side == 0 else has_up)
        def _():
            vx_copy(stage, side).start()

    def vx_wait(stage):
        @pl.when(has_down)
        def _():
            vx_copy(stage, 0).wait_send()
            vx_copy(stage, 1).wait_recv()

        @pl.when(has_up)
        def _():
            vx_copy(stage, 1).wait_send()
            vx_copy(stage, 0).wait_recv()

    def chunk_order(index):
        return (index + chunks - 1) % chunks

    vx_start(0, 0)
    vx_start(0, 1)

    @pl.loop(0, chunks)
    def _(index):
        px_start(0, chunk_order(index))

    load_cost.start()
    load_a2.start()

    sub = lax.broadcasted_iota(jnp.int32, (8, 128), 0)
    lane = lax.broadcasted_iota(jnp.int32, (8, 128), 1)
    sub_first, sub_last = sub == 0, sub == 7
    lane_first, lane_last = lane == 0, lane == 127

    load_a2.wait()
    a2_peak = jnp.max(jnp.abs(a2[...]), keepdims=True)
    a1_peak = jnp.max(jnp.abs(a1_v[...]), keepdims=True)
    load_value.wait()

    inner = jnp.logical_or(chip_x == 1, chip_x == 2)
    outer = jnp.logical_not(inner)

    def red_copy(stage, level, slot, sent, device):
        return pltpu.make_async_remote_copy(
            src_ref=red_s.at[stage, level],
            dst_ref=red_r.at[stage, slot],
            send_sem=red_send.at[stage, sent],
            recv_sem=red_recv.at[stage, slot],
            device_id=device,
            device_id_type=MESH,
        )

    def y_copies(stage):
        copies = [red_copy(stage, 0, 6, 6, partner)]
        for step in range(1, RING):
            for which in (0, 1):
                n = 2 * (step - 1)
                copies.append(
                    red_copy(stage, 0, n + core, n + which, along_y(step, which))
                )
        return copies

    def in_copies(stage):
        return [red_copy(stage, 1, 7, 7 + which, across(which)) for which in (0, 1)]

    def z_copies(stage):
        return [
            red_copy(stage, 2, 7 + step, 8 + step, along_z(step))
            for step in range(1, RING)
        ]

    def mirror_copies(stage):
        return [red_copy(stage, 3, 11, 12 + which, mirror(which)) for which in (0, 1)]

    def out_copies(stage):
        return [red_copy(stage, 4, 12, 14 + which, across(which)) for which in (0, 1)]

    sends_in = jnp.logical_and(outer, core == chip_x // 2)
    sends_mirror = jnp.logical_and(inner, core == chip_x // 2)
    sends_out = jnp.logical_and(inner, core == 1 - chip_x // 2)

    def start_all(copies):
        for copy in copies:
            copy.start()

    def take(stage, best, first, last):
        for slot in range(first, last):
            red_copy(stage, 0, slot, 0, partner).wait_recv()
            best = jnp.maximum(best, red_r[stage, slot])
        return best

    def all_max(stage, mine):
        red_s[stage, 0] = mine
        start_all(y_copies(stage))
        red_s[stage, 1] = take(stage, mine, 0, 7)

        @pl.when(sends_in)
        def _():
            start_all(in_copies(stage))

        @pl.when(inner)
        def _():
            best = take(stage, red_s[stage, 1], 7, 8)
            red_s[stage, 2] = best
            start_all(z_copies(stage))
            best = take(stage, best, 8, 11)
            red_s[stage, 3] = best

            @pl.when(sends_mirror)
            def _():
                start_all(mirror_copies(stage))

            red_s[stage, 4] = take(stage, best, 11, 12)

            @pl.when(sends_out)
            def _():
                start_all(out_copies(stage))

        @pl.when(outer)
        def _():
            red_s[stage, 4] = take(stage, red_s[stage, 1], 12, 13)

        return red_s[stage, 4]

    def all_max_drain(stage):
        for copy in y_copies(stage):
            copy.wait_send()
        for copies, sends in (
            (in_copies, sends_in),
            (z_copies, inner),
            (mirror_copies, sends_mirror),
            (out_copies, sends_out),
        ):

            @pl.when(sends)
            def _():
                for copy in copies(stage):
                    copy.wait_send()

    def row_neighbours(row):
        here = row + 1
        down = row + first_v * ((rows - 1 - row) // (rows - 1))
        up = row + 2 - last_v * (row // (rows - 1))
        return here, down, up

    def tile(s, c):
        return pl.ds(8 * s, 8), pl.ds(128 * c, 128)

    def row_maxima(field, row, carry):
        here, down, up = row_neighbours(row)
        m2, m3 = carry
        for plane in (1, 2):
            for c in range(tiles):
                cells = [field[(plane, here) + tile(s, c)] for s in range(strips)]
                turned = [pltpu.roll(x, 6, 0) for x in cells]
                for s in range(strips):
                    above = field[(plane, up) + tile(s, c)]
                    below = field[(plane, down) + tile(s, c)]
                    m2 = jnp.maximum(m2, jnp.abs(above - below))
                    if s < strips - 1:
                        ahead = jnp.where(sub >= 6, turned[s + 1], turned[s])
                    else:
                        ahead = jnp.where(sub >= 6, cells[s], turned[s])
                    m3 = jnp.maximum(m3, jnp.abs(ahead - cells[s]))
                step = jnp.abs(pltpu.roll(cells[0], 7, 0) - cells[0])
                m3 = jnp.maximum(m3, jnp.where(sub_first, step, 0.0))
                step = jnp.abs(pltpu.roll(cells[-1], 7, 0) - cells[-1])
                m3 = jnp.maximum(m3, jnp.where(sub == 6, step, 0.0))
        return m2, m3

    def add_maxima(field, first, last):
        def body(row, carry):
            return row_maxima(field, row, carry)

        peak[0], peak[1] = lax.fori_loop(first, last, body, (peak[0], peak[1]))

    def clear_maxima():
        peak[...] = jnp.zeros(peak.shape, jnp.float32)

    def spread(x):
        return jnp.broadcast_to(x, (8, 128))

    def make_coefficients(stage, best):
        m2, m3 = spread(best[0:1]), spread(best[1:2])
        push_limit = spread(best[2:3])
        if stage == 0:
            coef[7] = push_limit
        else:
            push_limit = coef[7]
        r2 = push_limit + (DISTURBANCE) + m2 * (1.0 / (2.0 * h2 * CONTROL_COST))
        r3 = (
            spread(a2_peak) + (DISTURBANCE) + m3 * (1.0 / (2.0 * h3 * CONTROL_COST))
        )
        courant = r1 / h1 + r2 / h2 + r3 / h3 + r4 / h1
        if stage % 2 == 0:
            dt = COURANT / courant
            coef[6] = dt
            centre = 1.0 + dt * courant
            scale = dt
        else:
            dt = coef[6]
            centre = 0.5 + 0.5 * (dt * courant)
            scale = 0.5 * dt
        k1 = scale * (1.0 / (2.0 * h1))
        k2 = scale * (1.0 / (2.0 * h2))
        k3 = scale * (1.0 / (2.0 * h3))
        coef[0] = k1
        coef[1] = k2
        coef[2] = k2 * r2
        coef[3] = k3 * (1.0 / (4.0 * h3 * CONTROL_COST))
        coef[4] = k3 * r3
        coef[5] = centre
        for s in range(strips):
            speed = (
                (2 * (sub + 8 * s) + 1 - tall).astype(jnp.float32)
                * (VELOCITY_LIMIT / tall)
            )
            tab_v[0, pl.ds(8 * s, 8)] = k1 * (speed + PLANNER_SPEED)
            tab_v[1, pl.ds(8 * s, 8)] = k1 * (speed - PLANNER_SPEED)
            for c in range(tiles):
                push = a2[tile(s, c)]
                tab_a[(0,) + tile(s, c)] = k3 * (push + DISTURBANCE)
                tab_a[(1,) + tile(s, c)] = k3 * (push - DISTURBANCE)

    def update_row(stage, row):
        field = fields[stage]
        here, down, up = row_neighbours(row)
        k1, k2 = coef[0], coef[1]
        e1, e4 = k1 * r1, k1 * r4
        q2 = k2 * (1.0 / (4.0 * h2 * CONTROL_COST))
        e2, q3, e3, centre = coef[2], coef[3], coef[4], coef[5]
        speed = (2 * (vx * rows + row) + 1 - total_vx).astype(jnp.float32) * (
            VELOCITY_LIMIT / total_vx
        )
        p1 = k1 * (speed + PLANNER_SPEED)
        n1 = k1 * (speed - PLANNER_SPEED)
        for plane in (1, 2):
            left = plane_low if plane == 1 else 1
            right = 2 if plane == 1 else plane_high
            push = a1_s[plane - 1, row]
            p2 = k2 * (push + DISTURBANCE)
            n2 = k2 * (push - DISTURBANCE)
            cells, ahead, behind = {}, {}, {}

            def fetch(s):
                for c in range(tiles):
                    x = field[(plane, here) + tile(s, c)]
                    cells[s, c] = x
                    ahead[s, c] = pltpu.roll(x, 7, 0)
                    behind[s, c] = pltpu.roll(x, 1, 0)

            fetch(0)
            for s in range(strips):
                if s + 1 < strips:
                    fetch(s + 1)
                lefts = [pltpu.roll(cells[s, c], 1, 1) for c in range(tiles)]
                rights = [pltpu.roll(cells[s, c], 127, 1) for c in range(tiles)]
                v_plus = tab_v[0, pl.ds(8 * s, 8)]
                v_minus = tab_v[1, pl.ds(8 * s, 8)]
                for c in range(tiles):
                    x = cells[s, c]
                    hi = field[(right, here) + tile(s, c)]
                    lo = field[(left, here) + tile(s, c)]
                    d = hi - lo
                    total = jnp.maximum(d * p1, d * n1) - e1 * (hi + lo)
                    hi = jnp.where(
                        lane_last, rights[c + 1] if c + 1 < tiles else x, rights[c]
                    )
                    lo = jnp.where(lane_first, lefts[c - 1] if c > 0 else x, lefts[c])
                    d = hi - lo
                    total += jnp.maximum(d * v_plus, d * v_minus) - e4 * (hi + lo)
                    hi = field[(plane, up) + tile(s, c)]
                    lo = field[(plane, down) + tile(s, c)]
                    d = hi - lo
                    total += d * (jnp.where(d > 0, p2, n2) - q2 * d) - e2 * (hi + lo)
                    hi = jnp.where(
                        sub_last,
                        ahead[s + 1, c] if s + 1 < strips else x,
                        ahead[s, c],
                    )
                    lo = jnp.where(
                        sub_first, behind[s - 1, c] if s > 0 else x, behind[s, c]
                    )
                    d = hi - lo
                    p3 = tab_a[(0,) + tile(s, c)]
                    n3 = tab_a[(1,) + tile(s, c)]
                    total += d * (jnp.where(d > 0, p3, n3) - q3 * d) - e3 * (hi + lo)
                    moved = centre * x + total
                    floor = cost[(plane - 1, row) + tile(s, c)]
                    if stage % 2 == 1:
                        base = fields[stage - 1][(plane, here) + tile(s, c)]
                        moved = 0.5 * base + moved
                    result = jnp.maximum(floor, moved)
                    if stage == 3:
                        out[(plane - 1, row) + tile(s, c)] = result
                        slot = plane - 1, slice(None), pl.ds(128 * c, 128)
                        fun_s[slot] = jnp.minimum(fun_s[slot], result)
                    else:
                        fields[stage + 1][(plane, here) + tile(s, c)] = result

    fun_s[...] = jnp.full(fun_s.shape, jnp.inf, jnp.float32)

    near_end = rows - CHUNK - 1
    clear_maxima()
    add_maxima(f0, 1, near_end)
    for stage in range(4):
        field = fields[stage]
        add_maxima(field, near_end, rows - 1)
        vx_wait(stage)
        add_maxima(field, 0, 1)
        add_maxima(field, rows - 1, rows)
        m2 = spread(jnp.max(peak[0], keepdims=True))
        m3 = spread(jnp.max(peak[1], keepdims=True))
        mine = jnp.where(sub == 0, m2, jnp.where(sub == 1, m3, spread(a1_peak)))
        best = all_max(stage, mine)
        make_coefficients(stage, best)
        clear_maxima()
        if stage == 0:
            load_cost.wait()

        @pl.loop(0, chunks)
        def _(index):
            chunk = chunk_order(index)
            px_wait_recv(stage, chunk)
            if stage > 0:
                px_wait_send(stage - 1, chunk)

            @pl.loop(0, CHUNK)
            def _(k):
                update_row(stage, chunk * CHUNK + k)

            if stage < 3:

                @pl.when(index > 0)
                def _():
                    px_start(stage + 1, chunk_order(index - 1))

                @pl.when(index == 1)
                def _():
                    vx_start(stage + 1, 1)

                @pl.when(index == 2)
                def _():
                    vx_start(stage + 1, 0)
                    if CHUNK > 1:
                        add_maxima(fields[stage + 1], 1, 2 * CHUNK - 1)

                @pl.when(index > 2)
                def _():
                    add_maxima(
                        fields[stage + 1], chunk * CHUNK - 1, chunk * CHUNK + CHUNK - 1
                    )

        if stage < 3:
            px_start(stage + 1, chunk_order(chunks - 1))
        all_max_drain(stage)

    def funnel_copy(step):
        return pltpu.make_async_remote_copy(
            src_ref=fun_s,
            dst_ref=fun_r.at[step - 1],
            send_sem=fun_send.at[step - 1],
            recv_sem=fun_recv.at[step - 1],
            device_id=(px, (vx + step) % nvx),
            device_id_type=MESH,
        )

    for step in range(1, RING):
        funnel_copy(step).start()

    @pl.loop(0, chunks)
    def _(index):
        px_wait_send(3, index)

    least = fun_s[...]
    for step in range(1, RING):
        funnel_copy(step).wait_recv()
        least = jnp.minimum(least, fun_r[step - 1])
    funnel[...] = jnp.min(least, axis=1)
    for step in range(1, RING):
        funnel_copy(step).wait_send()


def per_device(value_field, cost_field, accel_first, accel_second):
    cells_x, rows, tall, wide = value_field.shape
    field = pltpu.VMEM((cells_x + 2, rows + 2, tall, wide), jnp.float32)
    chunks = rows // CHUNK
    dma = pltpu.SemaphoreType.DMA
    hbm = pl.BlockSpec(memory_space=pl.ANY)
    vmem = pl.BlockSpec(memory_space=pltpu.VMEM)
    return pl.pallas_call(
        kernel,
        out_shape=(
            pltpu.VMEM(value_field.shape, jnp.float32),
            pltpu.VMEM((cells_x, wide), jnp.float32),
        ),
        in_specs=[pl.BlockSpec(memory_space=pltpu.SMEM), vmem, hbm, hbm, hbm],
        out_specs=(vmem, vmem),
        scratch_shapes=[
            field,
            field,
            field,
            field,
            pltpu.VMEM((cells_x, rows, tall, wide), jnp.float32),
            pltpu.VMEM((tall, wide), jnp.float32),
            pltpu.VMEM((2, tall, 128), jnp.float32),
            pltpu.VMEM((2, tall, wide), jnp.float32),
            pltpu.VMEM((4, 5, 8, 128), jnp.float32),
            pltpu.VMEM((4, 13, 8, 128), jnp.float32),
            pltpu.VMEM((2, 8, 128), jnp.float32),
            pltpu.VMEM((8, 8, 128), jnp.float32),
            pltpu.VMEM((cells_x, 8, wide), jnp.float32),
            pltpu.VMEM((RING - 1, cells_x, 8, wide), jnp.float32),
            dma((4, 2, chunks)),
            dma((4, 2, chunks)),
            dma((4, 2)),
            dma((4, 2)),
            dma((4, 16)),
            dma((4, 13)),
            dma((RING - 1,)),
            dma((RING - 1,)),
            dma((3,)),
        ],
        compiler_params=pltpu.CompilerParams(
            collective_id=0, has_side_effects=True, vmem_limit_bytes=56 * 1000 * 1000
        ),
    )(accel_first, accel_first, value_field, cost_field, accel_second)


def solution(mesh):
    placed = (P("px", "vx", None, None), P("px", "vx", None, None), P("px", "vx"), P())
    return jax.shard_map(
        per_device,
        mesh=mesh,
        in_specs=placed,
        out_specs=(P("px", "vx", None, None), P("px", None)),
        check_vma=False,
    )
```

```python
import functools

import jax
import jax.numpy as jnp
from jax import lax
from jax.experimental import pallas as pl
from jax.experimental.pallas import tpu as pltpu
from jax.sharding import PartitionSpec as P

MESH = pl.DeviceIdType.MESH
VELOCITY_LIMIT = 1.0
PLANNER_SPEED = 0.3
DISTURBANCE = 0.2
CONTROL_COST = 1.0
COURANT = 0.5
CHUNK = 2
RING = 4


def kernel(
    a1_hbm,
    value,
    cost_hbm,
    a2_hbm,
    out,
    funnel,
    f0,
    f1,
    f2,
    f3,
    cost,
    a1_s,
    a1_v,
    a2,
    tab_v,
    tab_a,
    red_s,
    red_r,
    peak,
    coef,
    least,
    fun_s,
    fun_r,
    px_send,
    px_recv,
    vx_send,
    vx_recv,
    red_send,
    red_recv,
    fun_send,
    fun_recv,
    load_sem,
):
    fields = (f0, f1, f2, f3)
    rows = cost.shape[1]
    tall = cost.shape[2]
    wide = cost.shape[3]
    strips = tall // 8
    tiles = wide // 128
    chunks = rows // CHUNK
    px, vx = lax.axis_index("px"), lax.axis_index("vx")
    npx, nvx = lax.axis_size("px"), lax.axis_size("vx")
    total_vx = rows * nvx
    h2 = 2.0 * VELOCITY_LIMIT / total_vx
    h3 = 2.0 * VELOCITY_LIMIT / tall
    h1 = h2 * h3
    r1 = VELOCITY_LIMIT * (total_vx - 1) / total_vx + PLANNER_SPEED
    r4 = VELOCITY_LIMIT * (tall - 1) / tall + PLANNER_SPEED

    core = px % 2
    chip_x = (px // 2) % RING
    chip_z = px // (2 * RING)
    has_left, has_right = px > 0, px < npx - 1
    has_down, has_up = vx > 0, vx < nvx - 1
    first_p = (npx - 1 - px) // (npx - 1)
    last_p = px // (npx - 1)
    first_v = (nvx - 1 - vx) // (nvx - 1)
    last_v = vx // (nvx - 1)
    plane_low = first_p
    plane_high = 3 - last_p

    def chip_device(x, y, z, which):
        return ((z * RING + x) * 2 + which, y)

    def across(which):
        return chip_device(chip_x + 1 - 2 * (chip_x % 2), vx, chip_z, which)

    def mirror(which):
        return chip_device(RING - 1 - chip_x, vx, chip_z, which)

    def along_y(step, which):
        return chip_device(chip_x, (vx + step) % RING, chip_z, which)

    def along_z(step):
        return chip_device(chip_x, vx, (chip_z + step) % RING, core)

    partner = (px + 1 - 2 * core, vx)

    load_value = pltpu.make_async_copy(
        value, f0.at[pl.ds(1, 2), pl.ds(1, rows)], load_sem.at[0]
    )
    load_cost = pltpu.make_async_copy(cost_hbm, cost, load_sem.at[1])
    load_a2 = pltpu.make_async_copy(a2_hbm, a2, load_sem.at[2])
    load_a1_s = pltpu.make_async_copy(a1_hbm, a1_s, load_sem.at[3])
    load_a1_v = pltpu.make_async_copy(a1_hbm, a1_v, load_sem.at[4])
    load_value.start()

    barrier = pltpu.get_barrier_semaphore()

    def greet(device):
        pl.semaphore_signal(barrier, inc=1, device_id=device, device_id_type=MESH)

    greet(partner)
    for which in (0, 1):
        greet(across(which))
        greet(mirror(which))
    for step in range(1, RING):
        greet(along_y(step, 0))
        greet(along_y(step, 1))
        greet(along_z(step))
    far_left = jnp.logical_and(jnp.logical_and(core == 0, chip_x == 0), has_left)
    far_right = jnp.logical_and(
        jnp.logical_and(core == 1, chip_x == RING - 1), has_right
    )

    @pl.when(far_left)
    def _():
        greet((px - 1, vx))

    @pl.when(far_right)
    def _():
        greet((px + 1, vx))

    far = far_left.astype(jnp.int32) + far_right.astype(jnp.int32)
    pl.semaphore_wait(barrier, 5 + 3 * (RING - 1) + far)

    def px_copy(stage, side, chunk):
        dst_plane = 3 if side == 0 else 0
        span = pl.ds(chunk * CHUNK + 1, CHUNK)
        if stage == 0:
            src = value.at[side, pl.ds(chunk * CHUNK, CHUNK)]
        else:
            src = fields[stage].at[1 + side, span]
        return pltpu.make_async_remote_copy(
            src_ref=src,
            dst_ref=fields[stage].at[dst_plane, span],
            send_sem=px_send.at[stage, side, chunk],
            recv_sem=px_recv.at[stage, side, chunk],
            device_id=(px - 1 if side == 0 else px + 1, vx),
            device_id_type=MESH,
        )

    def px_start(stage, chunk):
        @pl.when(has_left)
        def _():
            px_copy(stage, 0, chunk).start()

        @pl.when(has_right)
        def _():
            px_copy(stage, 1, chunk).start()

    def px_wait_send(stage, chunk):
        @pl.when(has_left)
        def _():
            px_copy(stage, 0, chunk).wait_send()

        @pl.when(has_right)
        def _():
            px_copy(stage, 1, chunk).wait_send()

    def px_wait_recv(stage, chunk):
        @pl.when(has_left)
        def _():
            px_copy(stage, 1, chunk).wait_recv()

        @pl.when(has_right)
        def _():
            px_copy(stage, 0, chunk).wait_recv()

    def vx_copy(stage, side):
        src_row = 1 if side == 0 else rows
        dst_row = rows + 1 if side == 0 else 0
        if stage == 0:
            src = value.at[:, pl.ds(src_row - 1, 1)]
        else:
            src = fields[stage].at[pl.ds(1, 2), pl.ds(src_row, 1)]
        return pltpu.make_async_remote_copy(
            src_ref=src,
            dst_ref=fields[stage].at[pl.ds(1, 2), pl.ds(dst_row, 1)],
            send_sem=vx_send.at[stage, side],
            recv_sem=vx_recv.at[stage, side],
            device_id=(px, vx - 1 if side == 0 else vx + 1),
            device_id_type=MESH,
        )

    def vx_start(stage, side):
        @pl.when(has_down if side == 0 else has_up)
        def _():
            vx_copy(stage, side).start()

    def vx_wait(stage):
        @pl.when(has_down)
        def _():
            vx_copy(stage, 0).wait_send()
            vx_copy(stage, 1).wait_recv()

        @pl.when(has_up)
        def _():
            vx_copy(stage, 1).wait_send()
            vx_copy(stage, 0).wait_recv()

    def chunk_order(index):
        return (index + chunks - 1) % chunks

    vx_start(0, 0)
    vx_start(0, 1)

    @pl.loop(0, chunks)
    def _(index):
        px_start(0, chunk_order(index))

    load_a1_v.start()
    load_a1_s.start()
    load_a2.start()
    load_cost.start()

    sub = lax.broadcasted_iota(jnp.int32, (8, 128), 0)
    lane = lax.broadcasted_iota(jnp.int32, (8, 128), 1)
    sub_first, sub_last = sub == 0, sub == 7
    lane_first, lane_last = lane == 0, lane == 127

    load_a2.wait()
    load_a1_v.wait()
    load_a1_s.wait()
    a2_peak = jnp.max(jnp.abs(a2[...]), keepdims=True)
    a1_peak = jnp.max(jnp.abs(a1_v[...]), keepdims=True)
    load_value.wait()

    inner = jnp.logical_or(chip_x == 1, chip_x == 2)
    outer = jnp.logical_not(inner)

    def red_copy(stage, level, slot, sent, device):
        return pltpu.make_async_remote_copy(
            src_ref=red_s.at[stage, level],
            dst_ref=red_r.at[stage, slot],
            send_sem=red_send.at[stage, sent],
            recv_sem=red_recv.at[stage, slot],
            device_id=device,
            device_id_type=MESH,
        )

    def y_copies(stage):
        copies = [red_copy(stage, 0, 6, 6, partner)]
        for step in range(1, RING):
            for which in (0, 1):
                n = 2 * (step - 1)
                copies.append(
                    red_copy(stage, 0, n + core, n + which, along_y(step, which))
                )
        return copies

    def in_copies(stage):
        return [red_copy(stage, 1, 7, 7 + which, across(which)) for which in (0, 1)]

    def z_copies(stage):
        return [
            red_copy(stage, 2, 7 + step, 8 + step, along_z(step))
            for step in range(1, RING)
        ]

    def mirror_copies(stage):
        return [red_copy(stage, 3, 11, 12 + which, mirror(which)) for which in (0, 1)]

    def out_copies(stage):
        return [red_copy(stage, 4, 12, 14 + which, across(which)) for which in (0, 1)]

    sends_in = jnp.logical_and(outer, core == chip_x // 2)
    sends_mirror = jnp.logical_and(inner, core == chip_x // 2)
    sends_out = jnp.logical_and(inner, core == 1 - chip_x // 2)

    def start_all(copies):
        for copy in copies:
            copy.start()

    def take(stage, best, first, last):
        for slot in range(first, last):
            red_copy(stage, 0, slot, 0, partner).wait_recv()
            best = jnp.maximum(best, red_r[stage, slot])
        return best

    def all_max(stage, mine):
        red_s[stage, 0] = mine
        start_all(y_copies(stage))
        red_s[stage, 1] = take(stage, mine, 0, 7)

        @pl.when(sends_in)
        def _():
            start_all(in_copies(stage))

        @pl.when(inner)
        def _():
            best = take(stage, red_s[stage, 1], 7, 8)
            red_s[stage, 2] = best
            start_all(z_copies(stage))
            best = take(stage, best, 8, 11)
            red_s[stage, 3] = best

            @pl.when(sends_mirror)
            def _():
                start_all(mirror_copies(stage))

            red_s[stage, 4] = take(stage, best, 11, 12)

            @pl.when(sends_out)
            def _():
                start_all(out_copies(stage))

        @pl.when(outer)
        def _():
            red_s[stage, 4] = take(stage, red_s[stage, 1], 12, 13)

        return red_s[stage, 4]

    def all_max_drain(stage):
        for copy in y_copies(stage):
            copy.wait_send()
        for copies, sends in (
            (in_copies, sends_in),
            (z_copies, inner),
            (mirror_copies, sends_mirror),
            (out_copies, sends_out),
        ):

            @pl.when(sends)
            def _():
                for copy in copies(stage):
                    copy.wait_send()

    def row_neighbours(row):
        here = row + 1
        down = row + first_v * ((rows - 1 - row) // (rows - 1))
        up = row + 2 - last_v * (row // (rows - 1))
        return here, down, up

    def tile(s, c):
        return pl.ds(8 * s, 8), pl.ds(128 * c, 128)

    def row_maxima(field, row, carry):
        here, down, up = row_neighbours(row)
        m2, m3 = carry
        for plane in (1, 2):
            for c in range(tiles):
                cells = [field[(plane, here) + tile(s, c)] for s in range(strips)]
                turned = [pltpu.roll(x, 6, 0) for x in cells]
                for s in range(strips):
                    above = field[(plane, up) + tile(s, c)]
                    below = field[(plane, down) + tile(s, c)]
                    m2 = jnp.maximum(m2, jnp.abs(above - below))
                    if s < strips - 1:
                        ahead = jnp.where(sub >= 6, turned[s + 1], turned[s])
                    else:
                        ahead = jnp.where(sub >= 6, cells[s], turned[s])
                    m3 = jnp.maximum(m3, jnp.abs(ahead - cells[s]))
                step = jnp.abs(pltpu.roll(cells[0], 7, 0) - cells[0])
                m3 = jnp.maximum(m3, jnp.where(sub_first, step, 0.0))
                step = jnp.abs(pltpu.roll(cells[-1], 7, 0) - cells[-1])
                m3 = jnp.maximum(m3, jnp.where(sub == 6, step, 0.0))
        return m2, m3

    def add_maxima(field, first, last):
        def body(row, carry):
            return row_maxima(field, row, carry)

        peak[0], peak[1] = lax.fori_loop(first, last, body, (peak[0], peak[1]))

    def clear_maxima():
        peak[...] = jnp.zeros(peak.shape, jnp.float32)

    def spread(x):
        return jnp.broadcast_to(x, (8, 128))

    def make_coefficients(stage, best):
        m2, m3 = spread(best[0:1]), spread(best[1:2])
        push_limit = spread(best[2:3])
        if stage == 0:
            coef[7] = push_limit
        else:
            push_limit = coef[7]
        r2 = push_limit + (DISTURBANCE) + m2 * (1.0 / (2.0 * h2 * CONTROL_COST))
        r3 = (
            spread(a2_peak) + (DISTURBANCE) + m3 * (1.0 / (2.0 * h3 * CONTROL_COST))
        )
        courant = r1 / h1 + r2 / h2 + r3 / h3 + r4 / h1
        if stage % 2 == 0:
            dt = COURANT / courant
            coef[6] = dt
            centre = 1.0 + dt * courant
            scale = dt
        else:
            dt = coef[6]
            centre = 0.5 + 0.5 * (dt * courant)
            scale = 0.5 * dt
        k1 = scale * (1.0 / (2.0 * h1))
        k2 = scale * (1.0 / (2.0 * h2))
        k3 = scale * (1.0 / (2.0 * h3))
        coef[0] = k1
        coef[1] = k2
        coef[2] = k2 * r2
        coef[3] = k3 * (1.0 / (4.0 * h3 * CONTROL_COST))
        coef[4] = k3 * r3
        coef[5] = centre
        for s in range(strips):
            speed = (
                (2 * (sub + 8 * s) + 1 - tall).astype(jnp.float32)
                * (VELOCITY_LIMIT / tall)
            )
            tab_v[0, pl.ds(8 * s, 8)] = k1 * (speed + PLANNER_SPEED)
            tab_v[1, pl.ds(8 * s, 8)] = k1 * (speed - PLANNER_SPEED)
            for c in range(tiles):
                push = a2[tile(s, c)]
                tab_a[(0,) + tile(s, c)] = k3 * (push + DISTURBANCE)
                tab_a[(1,) + tile(s, c)] = k3 * (push - DISTURBANCE)

    def update_row(stage, row):
        field = fields[stage]
        here, down, up = row_neighbours(row)
        k1, k2 = coef[0], coef[1]
        e1, e4 = k1 * r1, k1 * r4
        q2 = k2 * (1.0 / (4.0 * h2 * CONTROL_COST))
        e2, q3, e3, centre = coef[2], coef[3], coef[4], coef[5]
        speed = (2 * (vx * rows + row) + 1 - total_vx).astype(jnp.float32) * (
            VELOCITY_LIMIT / total_vx
        )
        p1 = k1 * (speed + PLANNER_SPEED)
        n1 = k1 * (speed - PLANNER_SPEED)
        for plane in (1, 2):
            left = plane_low if plane == 1 else 1
            right = 2 if plane == 1 else plane_high
            push = a1_s[plane - 1, row]
            p2 = k2 * (push + DISTURBANCE)
            n2 = k2 * (push - DISTURBANCE)
            cells, ahead, behind = {}, {}, {}

            def fetch(s):
                for c in range(tiles):
                    x = field[(plane, here) + tile(s, c)]
                    cells[s, c] = x
                    ahead[s, c] = pltpu.roll(x, 7, 0)
                    behind[s, c] = pltpu.roll(x, 1, 0)

            fetch(0)
            for s in range(strips):
                if s + 1 < strips:
                    fetch(s + 1)
                lefts = [pltpu.roll(cells[s, c], 1, 1) for c in range(tiles)]
                rights = [pltpu.roll(cells[s, c], 127, 1) for c in range(tiles)]
                v_plus = tab_v[0, pl.ds(8 * s, 8)]
                v_minus = tab_v[1, pl.ds(8 * s, 8)]
                for c in range(tiles):
                    x = cells[s, c]
                    hi = field[(right, here) + tile(s, c)]
                    lo = field[(left, here) + tile(s, c)]
                    d = hi - lo
                    total = jnp.maximum(d * p1, d * n1) - e1 * (hi + lo)
                    hi = jnp.where(
                        lane_last, rights[c + 1] if c + 1 < tiles else x, rights[c]
                    )
                    lo = jnp.where(lane_first, lefts[c - 1] if c > 0 else x, lefts[c])
                    d = hi - lo
                    total += jnp.maximum(d * v_plus, d * v_minus) - e4 * (hi + lo)
                    hi = field[(plane, up) + tile(s, c)]
                    lo = field[(plane, down) + tile(s, c)]
                    d = hi - lo
                    total += d * (jnp.where(d > 0, p2, n2) - q2 * d) - e2 * (hi + lo)
                    hi = jnp.where(
                        sub_last,
                        ahead[s + 1, c] if s + 1 < strips else x,
                        ahead[s, c],
                    )
                    lo = jnp.where(
                        sub_first, behind[s - 1, c] if s > 0 else x, behind[s, c]
                    )
                    d = hi - lo
                    p3 = tab_a[(0,) + tile(s, c)]
                    n3 = tab_a[(1,) + tile(s, c)]
                    total += d * (jnp.where(d > 0, p3, n3) - q3 * d) - e3 * (hi + lo)
                    moved = centre * x + total
                    floor = cost[(plane - 1, row) + tile(s, c)]
                    if stage % 2 == 1:
                        base = fields[stage - 1][(plane, here) + tile(s, c)]
                        moved = 0.5 * base + moved
                    result = jnp.maximum(floor, moved)
                    if stage == 3:
                        out[(plane - 1, row) + tile(s, c)] = result
                        slot = plane - 1, slice(None), pl.ds(128 * c, 128)
                        least[slot] = jnp.minimum(least[slot], result)
                    else:
                        fields[stage + 1][(plane, here) + tile(s, c)] = result

    least[...] = jnp.full(least.shape, jnp.inf, jnp.float32)

    near_end = rows - CHUNK - 1
    clear_maxima()
    add_maxima(f0, 1, near_end)
    for stage in range(4):
        field = fields[stage]
        add_maxima(field, near_end, rows - 1)
        vx_wait(stage)
        add_maxima(field, 0, 1)
        add_maxima(field, rows - 1, rows)
        m2 = spread(jnp.max(peak[0], keepdims=True))
        m3 = spread(jnp.max(peak[1], keepdims=True))
        mine = jnp.where(sub == 0, m2, jnp.where(sub == 1, m3, spread(a1_peak)))
        best = all_max(stage, mine)
        make_coefficients(stage, best)
        clear_maxima()
        if stage == 0:
            load_cost.wait()

        @pl.loop(0, chunks)
        def _(index):
            chunk = chunk_order(index)
            px_wait_recv(stage, chunk)
            if stage > 0:
                px_wait_send(stage - 1, chunk)

            @pl.loop(0, CHUNK)
            def _(k):
                update_row(stage, chunk * CHUNK + k)

            if stage < 3:

                @pl.when(index > 0)
                def _():
                    px_start(stage + 1, chunk_order(index - 1))

                @pl.when(index == 1)
                def _():
                    vx_start(stage + 1, 1)

                @pl.when(index == 2)
                def _():
                    vx_start(stage + 1, 0)
                    if CHUNK > 1:
                        add_maxima(fields[stage + 1], 1, 2 * CHUNK - 1)

                @pl.when(index > 2)
                def _():
                    add_maxima(
                        fields[stage + 1], chunk * CHUNK - 1, chunk * CHUNK + CHUNK - 1
                    )

        if stage < 3:
            px_start(stage + 1, chunk_order(chunks - 1))
            all_max_drain(stage)

    def funnel_copy(step):
        return pltpu.make_async_remote_copy(
            src_ref=fun_s,
            dst_ref=fun_r.at[step - 1],
            send_sem=fun_send.at[step - 1],
            recv_sem=fun_recv.at[step - 1],
            device_id=(px, (vx + step) % nvx),
            device_id_type=MESH,
        )

    fun_s[...] = jnp.min(least[...], axis=1)
    for step in (2, 1, 3):
        funnel_copy(step).start()

    @pl.loop(0, chunks)
    def _(index):
        px_wait_send(3, index)

    all_max_drain(3)
    lowest = fun_s[...]
    for step in range(1, RING):
        funnel_copy(step).wait_recv()
        lowest = jnp.minimum(lowest, fun_r[step - 1])
    funnel[...] = lowest
    for step in range(1, RING):
        funnel_copy(step).wait_send()


def store_kernel(field, funnel, field_out, funnel_out, sem):
    parts = 8
    rows = field.shape[1] // (parts // 2)
    copies = [
        pltpu.make_async_copy(
            field.at[n % 2, pl.ds(n // 2 * rows, rows)],
            field_out.at[n % 2, pl.ds(n // 2 * rows, rows)],
            sem.at[n],
        )
        for n in range(parts)
    ]
    copies.append(pltpu.make_async_copy(funnel, funnel_out, sem.at[parts]))
    for copy in copies:
        copy.start()
    for copy in copies:
        copy.wait()


def per_device(value_field, cost_field, accel_first, accel_second):
    cells_x, rows, tall, wide = value_field.shape
    field = pltpu.VMEM((cells_x + 2, rows + 2, tall, wide), jnp.float32)
    chunks = rows // CHUNK
    dma = pltpu.SemaphoreType.DMA
    hbm = pl.BlockSpec(memory_space=pl.ANY)
    vmem = pl.BlockSpec(memory_space=pltpu.VMEM)
    field_end, funnel = pl.pallas_call(
        kernel,
        out_shape=(
            pltpu.VMEM(value_field.shape, jnp.float32),
            pltpu.VMEM((cells_x, wide), jnp.float32),
        ),
        in_specs=[hbm, hbm, hbm, hbm],
        out_specs=(vmem, vmem),
        scratch_shapes=[
            field,
            field,
            field,
            field,
            pltpu.VMEM((cells_x, rows, tall, wide), jnp.float32),
            pltpu.SMEM((cells_x, rows), jnp.float32),
            pltpu.VMEM((cells_x, rows), jnp.float32),
            pltpu.VMEM((tall, wide), jnp.float32),
            pltpu.VMEM((2, tall, 128), jnp.float32),
            pltpu.VMEM((2, tall, wide), jnp.float32),
            pltpu.VMEM((4, 5, 8, 128), jnp.float32),
            pltpu.VMEM((4, 13, 8, 128), jnp.float32),
            pltpu.VMEM((2, 8, 128), jnp.float32),
            pltpu.VMEM((8, 8, 128), jnp.float32),
            pltpu.VMEM((cells_x, 8, wide), jnp.float32),
            pltpu.VMEM((cells_x, wide), jnp.float32),
            pltpu.VMEM((RING - 1, cells_x, wide), jnp.float32),
            dma((4, 2, chunks)),
            dma((4, 2, chunks)),
            dma((4, 2)),
            dma((4, 2)),
            dma((4, 16)),
            dma((4, 13)),
            dma((RING - 1,)),
            dma((RING - 1,)),
            dma((5,)),
        ],
        compiler_params=pltpu.CompilerParams(
            collective_id=0, has_side_effects=True, vmem_limit_bytes=56 * 1000 * 1000
        ),
    )(accel_first, value_field, cost_field, accel_second)
    return tuple(
        pl.pallas_call(
            store_kernel,
            out_shape=(
                jax.ShapeDtypeStruct(value_field.shape, jnp.float32),
                jax.ShapeDtypeStruct((cells_x, wide), jnp.float32),
            ),
            in_specs=[vmem, vmem],
            out_specs=(hbm, hbm),
            scratch_shapes=[dma((9,))],
            compiler_params=pltpu.CompilerParams(vmem_limit_bytes=1 << 20),
        )(
            pltpu.with_memory_space_constraint(field_end, pltpu.VMEM),
            pltpu.with_memory_space_constraint(funnel, pltpu.VMEM),
        )
    )


def solution(mesh):
    placed = (P("px", "vx", None, None), P("px", "vx", None, None), P("px", "vx"), P())
    return jax.shard_map(
        per_device,
        mesh=mesh,
        in_specs=placed,
        out_specs=(P("px", "vx", None, None), P("px", None)),
        check_vma=False,
    )
```

```python
import functools

import jax
import jax.numpy as jnp
from jax import lax
from jax.experimental import pallas as pl
from jax.experimental.pallas import tpu as pltpu
from jax.sharding import PartitionSpec as P

MESH = pl.DeviceIdType.MESH
VELOCITY_LIMIT = 1.0
PLANNER_SPEED = 0.3
DISTURBANCE = 0.2
CONTROL_COST = 1.0
COURANT = 0.5
BLOCK = 4
SIZES = (4, 4, 4, 2)
RING = 4


def kernel(
    a1_hbm,
    value,
    cost_hbm,
    a2_hbm,
    out,
    funnel,
    f0,
    f1,
    f2,
    f3,
    cost,
    a1_s,
    a1_v,
    a2,
    tab_v,
    tab_a,
    red_s,
    red_r,
    peak,
    coef,
    least,
    fun_s,
    fun_r,
    px_send,
    px_recv,
    vx_send,
    vx_recv,
    red_send,
    red_recv,
    fun_send,
    fun_recv,
    load_sem,
):
    fields = (f0, f1, f2, f3)
    rows = cost.shape[1]
    tall = cost.shape[2]
    wide = cost.shape[3]
    strips = tall // 8
    tiles = wide // 128
    px, vx = lax.axis_index("px"), lax.axis_index("vx")
    npx, nvx = lax.axis_size("px"), lax.axis_size("vx")
    total_vx = rows * nvx
    h2 = 2.0 * VELOCITY_LIMIT / total_vx
    h3 = 2.0 * VELOCITY_LIMIT / tall
    h1 = h2 * h3
    r1 = VELOCITY_LIMIT * (total_vx - 1) / total_vx + PLANNER_SPEED
    r4 = VELOCITY_LIMIT * (tall - 1) / tall + PLANNER_SPEED

    core = px % 2
    chip_x = (px // 2) % RING
    chip_z = px // (2 * RING)
    has_left, has_right = px > 0, px < npx - 1
    has_down, has_up = vx > 0, vx < nvx - 1
    first_p = (npx - 1 - px) // (npx - 1)
    last_p = px // (npx - 1)
    first_v = (nvx - 1 - vx) // (nvx - 1)
    last_v = vx // (nvx - 1)
    plane_low = first_p
    plane_high = 3 - last_p

    def chip_device(x, y, z, which):
        return ((z * RING + x) * 2 + which, y)

    def across(which):
        return chip_device(chip_x + 1 - 2 * (chip_x % 2), vx, chip_z, which)

    def mirror(which):
        return chip_device(RING - 1 - chip_x, vx, chip_z, which)

    def along_y(step, which):
        return chip_device(chip_x, (vx + step) % RING, chip_z, which)

    def along_z(step):
        return chip_device(chip_x, vx, (chip_z + step) % RING, core)

    partner = (px + 1 - 2 * core, vx)

    load_value = pltpu.make_async_copy(
        value, f0.at[pl.ds(1, 2), pl.ds(1, rows)], load_sem.at[0]
    )
    load_cost = pltpu.make_async_copy(cost_hbm, cost, load_sem.at[1])
    load_a2 = pltpu.make_async_copy(a2_hbm, a2, load_sem.at[2])
    load_a1_s = pltpu.make_async_copy(a1_hbm, a1_s, load_sem.at[3])
    load_a1_v = pltpu.make_async_copy(a1_hbm, a1_v, load_sem.at[4])
    load_value.start()

    barrier = pltpu.get_barrier_semaphore()

    def greet(device):
        pl.semaphore_signal(barrier, inc=1, device_id=device, device_id_type=MESH)

    greet(partner)
    for which in (0, 1):
        greet(across(which))
        greet(mirror(which))
    for step in range(1, RING):
        greet(along_y(step, 0))
        greet(along_y(step, 1))
        greet(along_z(step))
    far_left = jnp.logical_and(jnp.logical_and(core == 0, chip_x == 0), has_left)
    far_right = jnp.logical_and(
        jnp.logical_and(core == 1, chip_x == RING - 1), has_right
    )

    @pl.when(far_left)
    def _():
        greet((px - 1, vx))

    @pl.when(far_right)
    def _():
        greet((px + 1, vx))

    far = far_left.astype(jnp.int32) + far_right.astype(jnp.int32)
    pl.semaphore_wait(barrier, 5 + 3 * (RING - 1) + far)

    def px_copy(stage, side, chunk):
        dst_plane = 3 if side == 0 else 0
        size = SIZES[stage]
        span = pl.ds(chunk * size + 1, size)
        if stage == 0:
            src = value.at[side, pl.ds(chunk * size, size)]
        else:
            src = fields[stage].at[1 + side, span]
        return pltpu.make_async_remote_copy(
            src_ref=src,
            dst_ref=fields[stage].at[dst_plane, span],
            send_sem=px_send.at[stage, side, chunk],
            recv_sem=px_recv.at[stage, side, chunk],
            device_id=(px - 1 if side == 0 else px + 1, vx),
            device_id_type=MESH,
        )

    def px_start(stage, chunk):
        @pl.when(has_left)
        def _():
            px_copy(stage, 0, chunk).start()

        @pl.when(has_right)
        def _():
            px_copy(stage, 1, chunk).start()

    def px_wait_send(stage, chunk):
        @pl.when(has_left)
        def _():
            px_copy(stage, 0, chunk).wait_send()

        @pl.when(has_right)
        def _():
            px_copy(stage, 1, chunk).wait_send()

    def px_drain(stage):
        @pl.loop(0, rows // SIZES[stage])
        def _(chunk):
            px_wait_send(stage, chunk)

    def px_wait_recv(stage, chunk):
        @pl.when(has_left)
        def _():
            px_copy(stage, 1, chunk).wait_recv()

        @pl.when(has_right)
        def _():
            px_copy(stage, 0, chunk).wait_recv()

    def vx_copy(stage, side):
        src_row = 1 if side == 0 else rows
        dst_row = rows + 1 if side == 0 else 0
        if stage == 0:
            src = value.at[:, pl.ds(src_row - 1, 1)]
        else:
            src = fields[stage].at[pl.ds(1, 2), pl.ds(src_row, 1)]
        return pltpu.make_async_remote_copy(
            src_ref=src,
            dst_ref=fields[stage].at[pl.ds(1, 2), pl.ds(dst_row, 1)],
            send_sem=vx_send.at[stage, side],
            recv_sem=vx_recv.at[stage, side],
            device_id=(px, vx - 1 if side == 0 else vx + 1),
            device_id_type=MESH,
        )

    def vx_start(stage, side):
        @pl.when(has_down if side == 0 else has_up)
        def _():
            vx_copy(stage, side).start()

    def vx_wait(stage):
        @pl.when(has_down)
        def _():
            vx_copy(stage, 0).wait_send()
            vx_copy(stage, 1).wait_recv()

        @pl.when(has_up)
        def _():
            vx_copy(stage, 1).wait_send()
            vx_copy(stage, 0).wait_recv()

    def order(index, size):
        count = rows // size
        return (index + count - BLOCK // size) % count

    vx_start(0, 0)
    vx_start(0, 1)

    @pl.loop(0, rows // SIZES[0])
    def _(index):
        px_start(0, order(index, SIZES[0]))

    load_a1_v.start()
    load_a1_s.start()
    load_a2.start()
    load_cost.start()

    sub = lax.broadcasted_iota(jnp.int32, (8, 128), 0)
    lane = lax.broadcasted_iota(jnp.int32, (8, 128), 1)
    sub_first, sub_last = sub == 0, sub == 7
    lane_first, lane_last = lane == 0, lane == 127

    load_a2.wait()
    load_a1_v.wait()
    load_a1_s.wait()
    a2_peak = jnp.max(jnp.abs(a2[...]), keepdims=True)
    a1_peak = jnp.max(jnp.abs(a1_v[...]), keepdims=True)
    load_value.wait()

    inner = jnp.logical_or(chip_x == 1, chip_x == 2)
    outer = jnp.logical_not(inner)

    def red_copy(stage, level, slot, sent, device):
        return pltpu.make_async_remote_copy(
            src_ref=red_s.at[stage, level],
            dst_ref=red_r.at[stage, slot],
            send_sem=red_send.at[stage, sent],
            recv_sem=red_recv.at[stage, slot],
            device_id=device,
            device_id_type=MESH,
        )

    def y_copies(stage):
        copies = [red_copy(stage, 0, 6, 6, partner)]
        for step in range(1, RING):
            for which in (0, 1):
                n = 2 * (step - 1)
                copies.append(
                    red_copy(stage, 0, n + core, n + which, along_y(step, which))
                )
        return copies

    def in_copies(stage):
        return [red_copy(stage, 1, 7, 7 + which, across(which)) for which in (0, 1)]

    def z_copies(stage):
        return [
            red_copy(stage, 2, 7 + step, 8 + step, along_z(step))
            for step in range(1, RING)
        ]

    def mirror_copies(stage):
        return [red_copy(stage, 3, 11, 12 + which, mirror(which)) for which in (0, 1)]

    def out_copies(stage):
        return [red_copy(stage, 4, 12, 14 + which, across(which)) for which in (0, 1)]

    sends_in = jnp.logical_and(outer, core == chip_x // 2)
    sends_mirror = jnp.logical_and(inner, core == chip_x // 2)
    sends_out = jnp.logical_and(inner, core == 1 - chip_x // 2)

    def start_all(copies):
        for copy in copies:
            copy.start()

    def take(stage, best, first, last):
        for slot in range(first, last):
            red_copy(stage, 0, slot, 0, partner).wait_recv()
            best = jnp.maximum(best, red_r[stage, slot])
        return best

    def all_max(stage, mine):
        red_s[stage, 0] = mine
        start_all(y_copies(stage))
        red_s[stage, 1] = take(stage, mine, 0, 7)

        @pl.when(sends_in)
        def _():
            start_all(in_copies(stage))

        @pl.when(inner)
        def _():
            best = take(stage, red_s[stage, 1], 7, 8)
            red_s[stage, 2] = best
            start_all(z_copies(stage))
            best = take(stage, best, 8, 11)
            red_s[stage, 3] = best

            @pl.when(sends_mirror)
            def _():
                start_all(mirror_copies(stage))

            red_s[stage, 4] = take(stage, best, 11, 12)

            @pl.when(sends_out)
            def _():
                start_all(out_copies(stage))

        @pl.when(outer)
        def _():
            red_s[stage, 4] = take(stage, red_s[stage, 1], 12, 13)

        return red_s[stage, 4]

    def all_max_drain(stage):
        for copy in y_copies(stage):
            copy.wait_send()
        for copies, sends in (
            (in_copies, sends_in),
            (z_copies, inner),
            (mirror_copies, sends_mirror),
            (out_copies, sends_out),
        ):

            @pl.when(sends)
            def _():
                for copy in copies(stage):
                    copy.wait_send()

    def row_neighbours(row):
        here = row + 1
        down = row + first_v * ((rows - 1 - row) // (rows - 1))
        up = row + 2 - last_v * (row // (rows - 1))
        return here, down, up

    def tile(s, c):
        return pl.ds(8 * s, 8), pl.ds(128 * c, 128)

    def row_maxima(field, row, carry):
        here, down, up = row_neighbours(row)
        m2, m3 = carry
        for plane in (1, 2):
            for c in range(tiles):
                cells = [field[(plane, here) + tile(s, c)] for s in range(strips)]
                turned = [pltpu.roll(x, 6, 0) for x in cells]
                for s in range(strips):
                    above = field[(plane, up) + tile(s, c)]
                    below = field[(plane, down) + tile(s, c)]
                    m2 = jnp.maximum(m2, jnp.abs(above - below))
                    if s < strips - 1:
                        ahead = jnp.where(sub >= 6, turned[s + 1], turned[s])
                    else:
                        ahead = jnp.where(sub >= 6, cells[s], turned[s])
                    m3 = jnp.maximum(m3, jnp.abs(ahead - cells[s]))
                step = jnp.abs(pltpu.roll(cells[0], 7, 0) - cells[0])
                m3 = jnp.maximum(m3, jnp.where(sub_first, step, 0.0))
                step = jnp.abs(pltpu.roll(cells[-1], 7, 0) - cells[-1])
                m3 = jnp.maximum(m3, jnp.where(sub == 6, step, 0.0))
        return m2, m3

    def add_maxima(field, first, last):
        def body(row, carry):
            return row_maxima(field, row, carry)

        peak[0], peak[1] = lax.fori_loop(first, last, body, (peak[0], peak[1]))

    def clear_maxima():
        peak[...] = jnp.zeros(peak.shape, jnp.float32)

    def spread(x):
        return jnp.broadcast_to(x, (8, 128))

    def make_coefficients(stage, best):
        m2, m3 = spread(best[0:1]), spread(best[1:2])
        push_limit = spread(best[2:3])
        if stage == 0:
            coef[7] = push_limit
        else:
            push_limit = coef[7]
        r2 = push_limit + (DISTURBANCE) + m2 * (1.0 / (2.0 * h2 * CONTROL_COST))
        r3 = (
            spread(a2_peak) + (DISTURBANCE) + m3 * (1.0 / (2.0 * h3 * CONTROL_COST))
        )
        courant = r1 / h1 + r2 / h2 + r3 / h3 + r4 / h1
        if stage % 2 == 0:
            dt = COURANT / courant
            coef[6] = dt
            centre = 1.0 + dt * courant
            scale = dt
        else:
            dt = coef[6]
            centre = 0.5 + 0.5 * (dt * courant)
            scale = 0.5 * dt
        k1 = scale * (1.0 / (2.0 * h1))
        k2 = scale * (1.0 / (2.0 * h2))
        k3 = scale * (1.0 / (2.0 * h3))
        coef[0] = k1
        coef[1] = k2
        coef[2] = k2 * r2
        coef[3] = k3 * (1.0 / (4.0 * h3 * CONTROL_COST))
        coef[4] = k3 * r3
        coef[5] = centre
        for s in range(strips):
            speed = (
                (2 * (sub + 8 * s) + 1 - tall).astype(jnp.float32)
                * (VELOCITY_LIMIT / tall)
            )
            tab_v[0, pl.ds(8 * s, 8)] = k1 * (speed + PLANNER_SPEED)
            tab_v[1, pl.ds(8 * s, 8)] = k1 * (speed - PLANNER_SPEED)
            for c in range(tiles):
                push = a2[tile(s, c)]
                tab_a[(0,) + tile(s, c)] = k3 * (push + DISTURBANCE)
                tab_a[(1,) + tile(s, c)] = k3 * (push - DISTURBANCE)

    def update_row(stage, row):
        field = fields[stage]
        here, down, up = row_neighbours(row)
        k1, k2 = coef[0], coef[1]
        e1, e4 = k1 * r1, k1 * r4
        q2 = k2 * (1.0 / (4.0 * h2 * CONTROL_COST))
        e2, q3, e3, centre = coef[2], coef[3], coef[4], coef[5]
        speed = (2 * (vx * rows + row) + 1 - total_vx).astype(jnp.float32) * (
            VELOCITY_LIMIT / total_vx
        )
        p1 = k1 * (speed + PLANNER_SPEED)
        n1 = k1 * (speed - PLANNER_SPEED)
        for plane in (1, 2):
            left = plane_low if plane == 1 else 1
            right = 2 if plane == 1 else plane_high
            push = a1_s[plane - 1, row]
            p2 = k2 * (push + DISTURBANCE)
            n2 = k2 * (push - DISTURBANCE)
            cells, ahead, behind = {}, {}, {}

            def fetch(s):
                for c in range(tiles):
                    x = field[(plane, here) + tile(s, c)]
                    cells[s, c] = x
                    ahead[s, c] = pltpu.roll(x, 7, 0)
                    behind[s, c] = pltpu.roll(x, 1, 0)

            fetch(0)
            for s in range(strips):
                if s + 1 < strips:
                    fetch(s + 1)
                lefts = [pltpu.roll(cells[s, c], 1, 1) for c in range(tiles)]
                rights = [pltpu.roll(cells[s, c], 127, 1) for c in range(tiles)]
                v_plus = tab_v[0, pl.ds(8 * s, 8)]
                v_minus = tab_v[1, pl.ds(8 * s, 8)]
                for c in range(tiles):
                    x = cells[s, c]
                    hi = field[(right, here) + tile(s, c)]
                    lo = field[(left, here) + tile(s, c)]
                    d = hi - lo
                    total = jnp.maximum(d * p1, d * n1) - e1 * (hi + lo)
                    hi = jnp.where(
                        lane_last, rights[c + 1] if c + 1 < tiles else x, rights[c]
                    )
                    lo = jnp.where(lane_first, lefts[c - 1] if c > 0 else x, lefts[c])
                    d = hi - lo
                    total += jnp.maximum(d * v_plus, d * v_minus) - e4 * (hi + lo)
                    hi = field[(plane, up) + tile(s, c)]
                    lo = field[(plane, down) + tile(s, c)]
                    d = hi - lo
                    total += d * (jnp.where(d > 0, p2, n2) - q2 * d) - e2 * (hi + lo)
                    hi = jnp.where(
                        sub_last,
                        ahead[s + 1, c] if s + 1 < strips else x,
                        ahead[s, c],
                    )
                    lo = jnp.where(
                        sub_first, behind[s - 1, c] if s > 0 else x, behind[s, c]
                    )
                    d = hi - lo
                    p3 = tab_a[(0,) + tile(s, c)]
                    n3 = tab_a[(1,) + tile(s, c)]
                    total += d * (jnp.where(d > 0, p3, n3) - q3 * d) - e3 * (hi + lo)
                    moved = centre * x + total
                    floor = cost[(plane - 1, row) + tile(s, c)]
                    if stage % 2 == 1:
                        base = fields[stage - 1][(plane, here) + tile(s, c)]
                        moved = 0.5 * base + moved
                    result = jnp.maximum(floor, moved)
                    if stage == 3:
                        out[(plane - 1, row) + tile(s, c)] = result
                        slot = plane - 1, slice(None), pl.ds(128 * c, 128)
                        least[slot] = jnp.minimum(least[slot], result)
                    else:
                        fields[stage + 1][(plane, here) + tile(s, c)] = result

    least[...] = jnp.full(least.shape, jnp.inf, jnp.float32)

    near_end = rows - BLOCK - 1
    clear_maxima()
    add_maxima(f0, 1, near_end)
    for stage in range(4):
        field = fields[stage]
        size = SIZES[stage]
        block = BLOCK if stage < 3 else size
        blocks = rows // block
        add_maxima(field, near_end, rows - 1)
        vx_wait(stage)
        add_maxima(field, 0, 1)
        add_maxima(field, rows - 1, rows)
        m2 = spread(jnp.max(peak[0], keepdims=True))
        m3 = spread(jnp.max(peak[1], keepdims=True))
        mine = jnp.where(sub == 0, m2, jnp.where(sub == 1, m3, spread(a1_peak)))
        best = all_max(stage, mine)
        make_coefficients(stage, best)
        clear_maxima()
        if stage == 0:
            load_cost.wait()

        def send_block(index):
            sent = SIZES[stage + 1]
            for k in range(block // sent):
                px_start(stage + 1, order(index, block) * (block // sent) + k)

        @pl.loop(0, blocks)
        def _(index):
            first = order(index, block) * block
            for k in range(block // size):
                px_wait_recv(stage, order(index, block) * (block // size) + k)

            @pl.loop(0, block)
            def _(k):
                update_row(stage, first + k)

            if stage < 3:

                @pl.when(index > 0)
                def _():
                    send_block(index - 1)

                @pl.when(index == 1)
                def _():
                    vx_start(stage + 1, 1)

                @pl.when(index == 2)
                def _():
                    vx_start(stage + 1, 0)
                    add_maxima(fields[stage + 1], 1, 2 * block - 1)

                @pl.when(index > 2)
                def _():
                    add_maxima(fields[stage + 1], first - 1, first + block - 1)

        if stage < 3:
            send_block(blocks - 1)
            all_max_drain(stage)
        if stage > 0 and stage < 3:
            px_drain(stage - 1)

    def funnel_copy(step):
        return pltpu.make_async_remote_copy(
            src_ref=fun_s,
            dst_ref=fun_r.at[step - 1],
            send_sem=fun_send.at[step - 1],
            recv_sem=fun_recv.at[step - 1],
            device_id=(px, (vx + step) % nvx),
            device_id_type=MESH,
        )

    fun_s[...] = jnp.min(least[...], axis=1)
    for step in (2, 1, 3):
        funnel_copy(step).start()

    px_drain(2)
    px_drain(3)
    all_max_drain(3)
    lowest = fun_s[...]
    for step in range(1, RING):
        funnel_copy(step).wait_recv()
        lowest = jnp.minimum(lowest, fun_r[step - 1])
    funnel[...] = lowest
    for step in range(1, RING):
        funnel_copy(step).wait_send()


def store_kernel(field, funnel, field_out, funnel_out, sem):
    parts = 8
    rows = field.shape[1] // (parts // 2)
    copies = [
        pltpu.make_async_copy(
            field.at[n % 2, pl.ds(n // 2 * rows, rows)],
            field_out.at[n % 2, pl.ds(n // 2 * rows, rows)],
            sem.at[n],
        )
        for n in range(parts)
    ]
    copies.append(pltpu.make_async_copy(funnel, funnel_out, sem.at[parts]))
    for copy in copies:
        copy.start()
    for copy in copies:
        copy.wait()


def per_device(value_field, cost_field, accel_first, accel_second):
    cells_x, rows, tall, wide = value_field.shape
    field = pltpu.VMEM((cells_x + 2, rows + 2, tall, wide), jnp.float32)
    chunks = rows // min(SIZES)
    dma = pltpu.SemaphoreType.DMA
    hbm = pl.BlockSpec(memory_space=pl.ANY)
    vmem = pl.BlockSpec(memory_space=pltpu.VMEM)
    field_end, funnel = pl.pallas_call(
        kernel,
        out_shape=(
            pltpu.VMEM(value_field.shape, jnp.float32),
            pltpu.VMEM((cells_x, wide), jnp.float32),
        ),
        in_specs=[hbm, hbm, hbm, hbm],
        out_specs=(vmem, vmem),
        scratch_shapes=[
            field,
            field,
            field,
            field,
            pltpu.VMEM((cells_x, rows, tall, wide), jnp.float32),
            pltpu.SMEM((cells_x, rows), jnp.float32),
            pltpu.VMEM((cells_x, rows), jnp.float32),
            pltpu.VMEM((tall, wide), jnp.float32),
            pltpu.VMEM((2, tall, 128), jnp.float32),
            pltpu.VMEM((2, tall, wide), jnp.float32),
            pltpu.VMEM((4, 5, 8, 128), jnp.float32),
            pltpu.VMEM((4, 13, 8, 128), jnp.float32),
            pltpu.VMEM((2, 8, 128), jnp.float32),
            pltpu.VMEM((8, 8, 128), jnp.float32),
            pltpu.VMEM((cells_x, 8, wide), jnp.float32),
            pltpu.VMEM((cells_x, wide), jnp.float32),
            pltpu.VMEM((RING - 1, cells_x, wide), jnp.float32),
            dma((4, 2, chunks)),
            dma((4, 2, chunks)),
            dma((4, 2)),
            dma((4, 2)),
            dma((4, 16)),
            dma((4, 13)),
            dma((RING - 1,)),
            dma((RING - 1,)),
            dma((5,)),
        ],
        compiler_params=pltpu.CompilerParams(
            collective_id=0, has_side_effects=True, vmem_limit_bytes=56 * 1000 * 1000
        ),
    )(accel_first, value_field, cost_field, accel_second)
    return tuple(
        pl.pallas_call(
            store_kernel,
            out_shape=(
                jax.ShapeDtypeStruct(value_field.shape, jnp.float32),
                jax.ShapeDtypeStruct((cells_x, wide), jnp.float32),
            ),
            in_specs=[vmem, vmem],
            out_specs=(hbm, hbm),
            scratch_shapes=[dma((9,))],
            compiler_params=pltpu.CompilerParams(vmem_limit_bytes=1 << 20),
        )(
            pltpu.with_memory_space_constraint(field_end, pltpu.VMEM),
            pltpu.with_memory_space_constraint(funnel, pltpu.VMEM),
        )
    )


def solution(mesh):
    placed = (P("px", "vx", None, None), P("px", "vx", None, None), P("px", "vx"), P())
    return jax.shard_map(
        per_device,
        mesh=mesh,
        in_specs=placed,
        out_specs=(P("px", "vx", None, None), P("px", None)),
        check_vma=False,
    )
```
